512 devices in a mesh: gz: 32 (over z_lo, y), row: 16 (over z_hi, x, core).
Axes of the slice: x: 4, y: 4, z: 16 (z_hi: 2, z_lo: 8; z = z_hi * 8 + z_lo), core: 2. Of those that a mesh axis runs over, the one named last changes fastest.
Arguments:
- density: float32 [256, 128, 256], P('gz', 'row'), may hold values from 0.3 to 3
- pressure: float32 [256, 128, 256], P('gz', 'row'), may hold values from 0.3 to 3
- velocity: float32 [3, 256, 128, 256], P(None, 'gz', 'row'), may hold values from -3 to 3
- boundary: int32 [6], replicated, may hold values from 0 to 1
Outputs:
- density_out: float32 [256, 128, 256], P('gz', 'row')
- pressure_out: float32 [256, 128, 256], P('gz', 'row')
- velocity_out: float32 [3, 256, 128, 256], P(None, 'gz', 'row')
The draws below stay inside these ranges and needn't reach their ends.
Inputs may be any that keep to these rules, and one draw needn't show every extreme that they name: `boundary`: 1 marks a reflecting face, 0 an outflow face; entries 2k and 2k+1 are the lower and upper faces of x, y, z in turn.
All inputs are finite; a program needn't handle non-finite values.
Results may differ from the reference program's by a relative error of at most 0.0003.
Values sent between devices are 32-bit elements; how exact they have to be, the bound alone decides.
No kernel may reach another device: no remote copies, remote signals or barrier semaphores. Data moves between devices by JAX's collectives and lax.ppermute only.
A program may use at most 64 MiB of HBM per device.

```python
import math
import jax
import jax.numpy as jnp
import numpy as np
from jax import lax

NX = 256
RIEMANN_ITERS = 4
NY = 128
NZ = 256


def place_ends(entries, key, low, largest):
    longest = entries.shape.index(max(entries.shape))
    spots = []
    for shift in (0, 1):
        where = [jax.random.randint(jax.random.fold_in(key, axis), (), 0, length) for axis, length in enumerate(entries.shape)]
        where[longest] = (where[longest] + shift) % entries.shape[longest]
        spots.append(tuple(where))
    return entries.at[spots[0]].set(low).at[spots[1]].set(largest)


def level_of(stream_key, extent, pieces, low, high):
    factor_of = 1.0
    for dim, blocks in pieces:
        draws = jax.random.uniform(jax.random.fold_in(jax.random.fold_in(stream_key, 6), dim), (blocks,), jnp.float32, low / len(pieces), high / len(pieces))
        factor_of = factor_of * jnp.repeat(jnp.exp(draws), extent[dim] // blocks).reshape((-1,) + (1,) * (len(extent) - 1 - dim))
    return factor_of


def centred(rng, shape, deviation, most, pieces=(), held_as=jnp.bfloat16):
    result = deviation * jax.random.normal(rng, shape, jnp.float32)
    if pieces:
        result = result * level_of(rng, shape, pieces, -0.22, 0.18)
    return jnp.clip(result, -most, most).astype(held_as)


def setup_inputs(seed: int = 0) -> dict:
    arg_keys = jax.random.split(jax.random.key(seed), 5)
    density = jnp.clip(jnp.exp(math.log(3.0) - 2.3025851 * jax.random.uniform(arg_keys[0], (NZ, NY, NX), jnp.float32) ** level_of(arg_keys[0], (NZ, NY, NX), ((0, 32), (1, 16)), -0.2, 0.2)), 0.3, 3.0)
    pressure = jnp.clip(jnp.exp(math.log(3.0) - 2.3025851 * jax.random.uniform(arg_keys[1], (NZ, NY, NX), jnp.float32) ** level_of(arg_keys[1], (NZ, NY, NX), ((0, 32), (1, 16)), -0.2, 0.2)), 0.3, 3.0)
    velocity = centred(arg_keys[2], (3, NZ, NY, NX), 0.5, 3.0, ((1, 32), (2, 16)), jnp.float32)
    boundary = place_ends(jax.random.randint(arg_keys[3], (6,), 0, 2), jax.random.fold_in(arg_keys[3], 1), 0, 1).astype(jnp.int32)
    return {"density": density, "pressure": pressure, "velocity": velocity, "boundary": boundary}


gamma_gas = 1.4
courant_ratio = 0.05
dens_floor = 0.02
press_floor = 0.02
star_frac = 0.1

def mirror_sign(normal, ndim):
    table = np.ones(5, np.float32)
    table[normal] = -1.0
    return jnp.asarray(table.reshape((5,) + (1,) * (ndim - 1)))

def normal_mask(normal, ndim):
    table = np.zeros(3, np.float32)
    table[normal - 2] = 1.0
    return jnp.asarray(table.reshape((3,) + (1,) * (ndim - 1)))

def boundary_cells(interior, along, face_flag, at_lower, normal):
    reflect = jnp.flip(interior, axis=along) * mirror_sign(normal, interior.ndim)
    edge_index = 0 if at_lower else 2
    edge_cell = lax.slice_in_dim(interior, edge_index, edge_index + 1, axis=along)
    outflow = jnp.concatenate([edge_cell, edge_cell, edge_cell], axis=along)
    return jnp.where(face_flag == 1, reflect, outflow)

def add_ghosts(fields, along, low_flag, high_flag, normal):
    inner_len = fields.shape[along]
    lower_ghosts = boundary_cells(lax.slice_in_dim(fields, 0, 3, axis=along), along, low_flag, True, normal)
    upper_ghosts = boundary_cells(lax.slice_in_dim(fields, inner_len - 3, inner_len, axis=along), along, high_flag, False, normal)
    return jnp.concatenate([lower_ghosts, fields, upper_ghosts], axis=along)

def conserved(prims):
    dens = prims[0:1]
    speeds = prims[2:5]
    energy = prims[1:2] / (gamma_gas - 1.0) + 0.5 * dens * lax.optimization_barrier(jnp.sum(speeds * speeds, axis=0, keepdims=True))
    return jnp.concatenate([dens, energy, dens * speeds], axis=0)

def primitive(conserv):
    dens = jnp.maximum(conserv[0:1], dens_floor)
    speeds = conserv[2:5] / dens
    press = (gamma_gas - 1.0) * (conserv[1:2] - 0.5 * dens * lax.optimization_barrier(jnp.sum(speeds * speeds, axis=0, keepdims=True)))
    return jnp.concatenate([dens, jnp.maximum(press, press_floor), speeds], axis=0)

def shock_side(star_press, side_press, sound_imp):
    ratio_g = (gamma_gas + 1.0) / (2.0 * gamma_gas)
    wave_speed = sound_imp * jnp.sqrt(1.0 + ratio_g * (star_press / side_press - 1.0))
    jump_speed = (star_press - side_press) / wave_speed
    jump_slope = sound_imp * sound_imp * (1.0 + ratio_g * (star_press - side_press) / (2.0 * side_press)) / wave_speed ** 3
    return (jump_speed, jump_slope)

def godunov(left_state, right_state, normal):
    dens_left, dens_right = (left_state[0], right_state[0])
    press_left, press_right = (left_state[1], right_state[1])
    normal_left, normal_right = (left_state[normal], right_state[normal])
    sound_left = jnp.sqrt(gamma_gas * press_left * dens_left)
    sound_right = jnp.sqrt(gamma_gas * press_right * dens_right)
    floor_press = star_frac * jnp.minimum(press_left, press_right)
    star_press = (sound_right * press_left + sound_left * press_right - sound_left * sound_right * (normal_right - normal_left)) / (sound_left + sound_right)
    star_press = jnp.maximum(star_press, floor_press)
    for attempt in range(RIEMANN_ITERS):
        jump_left, slope_left = shock_side(star_press, press_left, sound_left)
        jump_right, slope_right = shock_side(star_press, press_right, sound_right)
        star_press = star_press - (normal_right - normal_left + jump_left + jump_right) / (slope_left + slope_right)
        star_press = jnp.maximum(star_press, floor_press)
    jump_left, slope_left = shock_side(star_press, press_left, sound_left)
    jump_right, slope_right = shock_side(star_press, press_right, sound_right)
    star_speed = 0.5 * (normal_left - jump_left + (normal_right + jump_right))
    upwind = star_speed > 0.0
    dens_up = jnp.where(upwind, dens_left, dens_right)
    press_up = jnp.where(upwind, press_left, press_right)
    selector = normal_mask(normal, left_state.ndim)
    vel_up = jnp.where(upwind[None], left_state[2:5], right_state[2:5])
    vel_up = selector * star_speed[None] + (1.0 - selector) * vel_up
    energy_up = press_up / (gamma_gas - 1.0) + 0.5 * dens_up * lax.optimization_barrier(jnp.sum(vel_up * vel_up, axis=0))
    mass_flux = dens_up * star_speed
    energy_flux = (energy_up + star_press) * star_speed
    moment_flux = mass_flux[None] * vel_up + selector * star_press[None]
    return jnp.concatenate([mass_flux[None], energy_flux[None], moment_flux], axis=0)

def sweep_cells(padded, along, normal):
    inner_len = padded.shape[along] - 6

    def window(start, length):
        return lax.slice_in_dim(padded, start, start + length, axis=along)
    left_in = window(1, inner_len + 3)
    right_in = window(2, inner_len + 3)
    interfaces = (7.0 * (left_in + right_in) - (window(0, inner_len + 3) + window(3, inner_len + 3))) / 12.0
    interfaces = jnp.clip(interfaces, jnp.minimum(left_in, right_in), jnp.maximum(left_in, right_in))
    centres = window(2, inner_len + 2)
    to_left = lax.slice_in_dim(interfaces, 0, inner_len + 2, axis=along) - centres
    to_right = lax.slice_in_dim(interfaces, 1, inner_len + 3, axis=along) - centres
    west_edge = centres + jnp.clip(to_left, -2.0 * jnp.abs(to_right), 2.0 * jnp.abs(to_right))
    east_edge = centres + jnp.clip(to_right, -2.0 * jnp.abs(to_left), 2.0 * jnp.abs(to_left))
    left_state = lax.slice_in_dim(east_edge, 0, inner_len + 1, axis=along)
    right_state = lax.slice_in_dim(west_edge, 1, inner_len + 2, axis=along)
    fluxes = godunov(left_state, right_state, normal)
    conserv = conserved(window(3, inner_len))
    conserv = conserv - courant_ratio * (lax.slice_in_dim(fluxes, 1, inner_len + 1, axis=along) - lax.slice_in_dim(fluxes, 0, inner_len, axis=along))
    return primitive(conserv)

def reference(density, pressure, velocity, boundary):
    fields = jnp.concatenate([density[None], pressure[None], velocity], axis=0)
    planes = jnp.transpose(fields, (1, 0, 2, 3))

    def xy_sweeps(plane_cut):
        plane_cut = sweep_cells(add_ghosts(plane_cut, 2, boundary[0], boundary[1], 2), 2, 2)
        return sweep_cells(add_ghosts(plane_cut, 1, boundary[2], boundary[3], 3), 1, 3)
    planes = lax.map(xy_sweeps, planes)
    row_cuts = jnp.transpose(planes, (2, 1, 0, 3))

    def z_sweep(column_cut):
        return sweep_cells(add_ghosts(column_cut, 1, boundary[4], boundary[5], 4), 1, 4)
    row_cuts = lax.map(z_sweep, row_cuts)
    fields = jnp.transpose(row_cuts, (1, 2, 0, 3))
    return (fields[0], fields[1], fields[2:5])
```

```python
import functools

import jax
import jax.numpy as jnp
from jax import lax
from jax.experimental import pallas as pl
from jax.experimental.pallas import tpu as pltpu
from jax.sharding import PartitionSpec as P

RIEMANN_ITERS = 4
GAMMA = 1.4
COURANT = 0.05
DENS_FLOOR = 0.02
PRESS_FLOOR = 0.02
STAR_FRAC = 0.1
RATIO_G = (GAMMA + 1.0) / (2.0 * GAMMA)
WIDTH = 3
LANES = 128


def face_value(far_left, left, right, far_right):
    value = (7.0 / 12.0) * (left + right) - (1.0 / 12.0) * (far_left + far_right)
    return jnp.clip(value, jnp.minimum(left, right), jnp.maximum(left, right))


def cell_edges(cell, face_left, face_right):
    to_left = face_left - cell
    to_right = face_right - cell
    two_left = 2.0 * jnp.abs(to_left)
    two_right = 2.0 * jnp.abs(to_right)
    west = cell + jnp.clip(to_left, -two_right, two_right)
    east = cell + jnp.clip(to_right, -two_left, two_left)
    return west, east


def godunov(left, right):
    rho_l, p_l, u_l, s_l, t_l = left
    rho_r, p_r, u_r, s_r, t_r = right
    inv_l = lax.rsqrt(GAMMA * (p_l * rho_l))
    inv_r = lax.rsqrt(GAMMA * (p_r * rho_r))
    jump = u_r - u_l
    floor = STAR_FRAC * jnp.minimum(p_l, p_r)
    star = (inv_l * p_l + inv_r * p_r - jump) / (inv_l + inv_r)
    star = jnp.maximum(star, floor)
    slope_l = RATIO_G / p_l
    slope_r = RATIO_G / p_r

    def side(star, p, inv, slope):
        root = lax.rsqrt((1.0 - RATIO_G) + slope * star)
        scaled = inv * root
        return root, scaled, (star - p) * scaled

    for _ in range(RIEMANN_ITERS):
        root_l, scaled_l, f_l = side(star, p_l, inv_l, slope_l)
        root_r, scaled_r, f_r = side(star, p_r, inv_r, slope_r)
        twice = scaled_l * (1.0 + root_l * root_l) + scaled_r * (1.0 + root_r * root_r)
        star = star - 2.0 * (jump + f_l + f_r) / twice
        star = jnp.maximum(star, floor)
    _, _, f_l = side(star, p_l, inv_l, slope_l)
    _, _, f_r = side(star, p_r, inv_r, slope_r)
    speed = 0.5 * ((u_l - f_l) + (u_r + f_r))
    upwind = speed > 0.0
    rho = jnp.where(upwind, rho_l, rho_r)
    p = jnp.where(upwind, p_l, p_r)
    s = jnp.where(upwind, s_l, s_r)
    t = jnp.where(upwind, t_l, t_r)
    mass = rho * speed
    energy = p * (1.0 / (GAMMA - 1.0)) + 0.5 * rho * (speed * speed + s * s + t * t)
    return (mass, (energy + star) * speed, mass * speed + star, mass * s, mass * t)


def advance(cell, flux_low, flux_high):
    rho, p, u, s, t = cell
    change = [COURANT * (high - low) for low, high in zip(flux_low, flux_high)]
    mass = rho - change[0]
    energy = p * (1.0 / (GAMMA - 1.0)) + 0.5 * rho * (u * u + s * s + t * t) - change[1]
    mom = [rho * v - c for v, c in zip((u, s, t), change[2:])]
    rho = jnp.maximum(mass, DENS_FLOOR)
    inv = 1.0 / rho
    u, s, t = (m * inv for m in mom)
    p = (GAMMA - 1.0) * (energy - 0.5 * rho * (u * u + s * s + t * t))
    return rho, jnp.maximum(p, PRESS_FLOOR), u, s, t


def field_order(normal):
    return (0, 1, normal) + tuple(v for v in (2, 3, 4) if v != normal)


def sign_of(flag):
    return jnp.where(flag == 1, -1.0, 1.0).astype(jnp.float32)


def x_kernel(
    flags, index, dens, press, vel, main, first, second, left, right, turn
):
    planes, rows, cells = dens.shape
    pair = 2
    half = cells // LANES
    lane = lax.broadcasted_iota(jnp.int32, (pair * rows, cells), 1)
    short = lax.broadcasted_iota(jnp.int32, (rows, LANES), 1)
    sign_low, sign_high = sign_of(flags[0]), sign_of(flags[1])

    def load(field, start):
        ref = (dens, press, vel.at[0], vel.at[1], vel.at[2])[field]
        return ref[start : start + pair].reshape(pair * rows, cells)

    edge = [jnp.zeros((rows, LANES), jnp.float32) for _ in range(5)]
    for start in range(0, planes, pair):
        block = slice(start * rows, (start + pair) * rows)
        for field in range(5):
            low = sign_low if field == 2 else 1.0
            high = sign_high if field == 2 else 1.0
            cell = load(field, start)
            before = jnp.where(lane == 0, low * cell, pltpu.roll(cell, 1, 1))
            after = jnp.where(lane == cells - 1, high * cell, pltpu.roll(cell, cells - 1, 1))
            face = face_value(pltpu.roll(before, 1, 1), before, cell, after)
            face = jnp.where(lane == 0, 0.5 * (before + cell), face)
            face_next = jnp.where(
                lane == cells - 1, 0.5 * (cell + after), pltpu.roll(face, cells - 1, 1)
            )
            west, east = cell_edges(cell, face, face_next)
            left[field, block, :] = jnp.where(lane == 0, low * west, pltpu.roll(east, 1, 1))
            right[field, block, :] = west
            for k in range(pair):
                z = start + k
                last = east[k * rows : (k + 1) * rows, cells - LANES :]
                edge[field] = jnp.where(short == z, pltpu.roll(last, z + 1, 1), edge[field])
    wall = [jnp.where(short < planes, e, 1.0) for e in edge]
    wall_flux = godunov(wall, [w * sign_high if f == 2 else w for f, w in enumerate(wall)])

    for start in range(0, planes, pair):
        block = slice(start * rows, (start + pair) * rows)
        flux = godunov(
            [left[f, block, :] for f in range(5)], [right[f, block, :] for f in range(5)]
        )
        after = []
        for f in range(5):
            rolled = pltpu.roll(flux[f], cells - 1, 1)
            end = jnp.concatenate(
                [pltpu.roll(wall_flux[f], LANES - 1 - start - k, 1) for k in range(pair)], axis=0
            )
            tail = jnp.where(short_pair(short, pair) == LANES - 1, end, rolled[:, cells - LANES :])
            after.append(jnp.concatenate([rolled[:, : cells - LANES], tail], axis=1))
        new = advance([load(f, start) for f in range(5)], flux, after)
        for f in range(5):
            for h in range(half):
                base = ((f * half + h) * planes + start) * rows
                turn[base : base + pair * rows, :] = new[f][:, h * LANES : (h + 1) * LANES]
    turn_over(turn, main, half)
    edge_blocks(index[0], main, first, second)


def short_pair(short, pair):
    return jnp.concatenate([short] * pair, axis=0)


def turn_over(turn, main, half):
    fields, outer, inner, _ = main.shape
    for f in range(fields):
        for h in range(half):
            base = (f * half + h) * outer * inner
            for j in range(outer):
                main[f, j, :, h * LANES : (h + 1) * LANES] = turn[pl.ds(base + j, inner, stride=outer), :]


def edge_blocks(place, main, first, second):
    outer = main.shape[1]
    odd = lax.rem(place, 2) == 1
    start_first = jnp.where(odd, outer - WIDTH, 0)
    start_second = jnp.where(odd, 0, outer - WIDTH)
    for f in range(5):
        for k in range(WIDTH):
            first[f, k] = main[f, start_first + k]
            second[f, k] = main[f, start_second + k]


def sweep_outer(place, count, flag_low, flag_high, normal, main, first, second, ghost, left, right, flux, store):
    outer, rows, cells = main.shape[1:]
    half = cells // LANES
    odd = lax.rem(place, 2) == 1

    @pl.when(odd)
    def _():
        ghost[:, :WIDTH] = second[...]
        ghost[:, WIDTH:] = first[...]

    @pl.when(jnp.logical_not(odd))
    def _():
        ghost[:, :WIDTH] = first[...]
        ghost[:, WIDTH:] = second[...]

    def wall(slot, edge, step, flag):
        for f in range(5):
            sign = sign_of(flag) if f == normal else 1.0
            for k in range(WIDTH):
                ghost[f, slot(k)] = jnp.where(flag == 1, sign * main[f, edge + step * k], main[f, edge])

    @pl.when(place == 0)
    def _():
        wall(lambda k: WIDTH - 1 - k, 0, 1, flag_low)

    @pl.when(place == count - 1)
    def _():
        wall(lambda k: WIDTH + k, outer - 1, -1, flag_high)

    order = field_order(normal)
    for f in range(5):
        for h in range(half):
            part = slice(h * LANES, (h + 1) * LANES)

            def cell(i):
                if i < 0:
                    return ghost[f, WIDTH + i, :, part]
                if i >= outer:
                    return ghost[f, WIDTH + i - outer, :, part]
                return main[f, i, :, part]

            value = {i: cell(i) for i in range(-WIDTH, outer + WIDTH)}
            face = None
            for i in range(-1, outer + 1):
                if face is None:
                    face = face_value(*(value[i + d] for d in (-2, -1, 0, 1)))
                face_next = face_value(*(value[i + d] for d in (-1, 0, 1, 2)))
                west, east = cell_edges(value[i], face, face_next)
                if i < outer:
                    left[f, i + 1, :, part] = east
                if i >= 0:
                    right[f, i, :, part] = west
                face = face_next
    chunk = 3
    for start in range(0, outer + 1, chunk):
        stop = min(start + chunk, outer + 1)
        for h in range(half):
            part = slice(h * LANES, (h + 1) * LANES)
            out = godunov(
                [left[f, start:stop, :, part] for f in order],
                [right[f, start:stop, :, part] for f in order],
            )
            for f in range(5):
                flux[f, start:stop, :, part] = out[f]
    for i in range(outer):
        new = advance(
            [main[f, i] for f in order], [flux[f, i] for f in range(5)], [flux[f, i + 1] for f in range(5)]
        )
        store(i, {f: new[k] for k, f in enumerate(order)})


def y_kernel(flags, index, main, first, second, out, out_first, out_second, ghost, left, right, flux, turn, *, count):
    outer, rows, cells = main.shape[1:]
    half = cells // LANES

    def store(i, new):
        for f in range(5):
            for h in range(half):
                base = ((f * half + h) * outer + i) * rows
                turn[base : base + rows, :] = new[f][:, h * LANES : (h + 1) * LANES]

    sweep_outer(index[0], count, flags[2], flags[3], 3, main, first, second, ghost, left, right, flux, store)
    turn_over(turn, out, half)
    edge_blocks(index[1], out, out_first, out_second)


def z_kernel(flags, index, main, first, second, dens, press, vel, ghost, left, right, flux, *, count):
    def store(i, new):
        dens[i] = new[0]
        press[i] = new[1]
        for v in range(3):
            vel[v, i] = new[2 + v]

    sweep_outer(index[1], count, flags[4], flags[5], 4, main, first, second, ghost, left, right, flux, store)


def exchange(block, axis, start):
    pairs = []
    for i in range(start, lax.axis_size(axis) - 1, 2):
        pairs += [(i, i + 1), (i + 1, i)]
    return lax.ppermute(block, axis, pairs)


def on_device(density, pressure, velocity, boundary):
    planes, rows, cells = density.shape
    half = cells // LANES
    f32 = jnp.float32
    place = jnp.stack([lax.axis_index("row"), lax.axis_index("gz")]).astype(jnp.int32)
    smem = pl.BlockSpec(memory_space=pltpu.SMEM)
    vmem = pl.BlockSpec(memory_space=pltpu.VMEM)
    params = pltpu.CompilerParams(vmem_limit_bytes=32 << 20)
    by_y = jax.ShapeDtypeStruct((5, rows, planes, cells), f32)
    by_z = jax.ShapeDtypeStruct((5, planes, rows, cells), f32)
    y_edge = jax.ShapeDtypeStruct((5, WIDTH, planes, cells), f32)
    z_edge = jax.ShapeDtypeStruct((5, WIDTH, rows, cells), f32)
    turn = pltpu.VMEM((5 * half * planes * rows, LANES), f32)

    def work(outer, inner):
        return [
            pltpu.VMEM((5, 2 * WIDTH, inner, cells), f32),
            pltpu.VMEM((5, outer + 1, inner, cells), f32),
            pltpu.VMEM((5, outer + 1, inner, cells), f32),
            pltpu.VMEM((5, outer + 1, inner, cells), f32),
        ]

    main, first, second = pl.pallas_call(
        x_kernel,
        out_shape=(by_y, y_edge, y_edge),
        in_specs=[smem, smem, vmem, vmem, vmem],
        out_specs=(vmem, vmem, vmem),
        scratch_shapes=[
            pltpu.VMEM((5, planes * rows, cells), f32),
            pltpu.VMEM((5, planes * rows, cells), f32),
            turn,
        ],
        compiler_params=params,
        name="x_sweep",
    )(boundary, place, density, pressure, velocity)
    first = exchange(first, "row", 1)
    second = exchange(second, "row", 0)
    main, first, second = pl.pallas_call(
        functools.partial(y_kernel, count=lax.axis_size("row")),
        out_shape=(by_z, z_edge, z_edge),
        in_specs=[smem, smem, vmem, vmem, vmem],
        out_specs=(vmem, vmem, vmem),
        scratch_shapes=work(rows, planes) + [turn],
        compiler_params=params,
        name="y_sweep",
    )(boundary, place, main, first, second)
    first = exchange(first, "gz", 1)
    second = exchange(second, "gz", 0)
    return pl.pallas_call(
        functools.partial(z_kernel, count=lax.axis_size("gz")),
        out_shape=(
            jax.ShapeDtypeStruct(density.shape, f32),
            jax.ShapeDtypeStruct(pressure.shape, f32),
            jax.ShapeDtypeStruct(velocity.shape, f32),
        ),
        in_specs=[smem, smem, vmem, vmem, vmem],
        out_specs=(vmem, vmem, vmem),
        scratch_shapes=work(planes, rows),
        compiler_params=params,
        name="z_sweep",
    )(boundary, place, main, first, second)


def solution(mesh):
    in_specs = (P("gz", "row", None), P("gz", "row", None), P(None, "gz", "row", None), P())
    out_specs = (P("gz", "row", None), P("gz", "row", None), P(None, "gz", "row", None))
    return jax.shard_map(
        on_device, mesh=mesh, in_specs=in_specs, out_specs=out_specs, check_vma=False
    )
```

```python
import functools

import jax
import jax.numpy as jnp
from jax import lax
from jax.experimental import pallas as pl
from jax.experimental.pallas import tpu as pltpu
from jax.sharding import PartitionSpec as P

RIEMANN_ITERS = 4
GAMMA = 1.4
COURANT = 0.05
DENS_FLOOR = 0.02
PRESS_FLOOR = 0.02
STAR_FRAC = 0.1
RATIO_G = (GAMMA + 1.0) / (2.0 * GAMMA)
WIDTH = 3
LANES = 128


def face_value(far_left, left, right, far_right):
    value = (7.0 / 12.0) * (left + right) - (1.0 / 12.0) * (far_left + far_right)
    return jnp.clip(value, jnp.minimum(left, right), jnp.maximum(left, right))


def cell_edges(cell, face_left, face_right):
    to_left = face_left - cell
    to_right = face_right - cell
    two_left = 2.0 * jnp.abs(to_left)
    two_right = 2.0 * jnp.abs(to_right)
    west = cell + jnp.clip(to_left, -two_right, two_right)
    east = cell + jnp.clip(to_right, -two_left, two_left)
    return west, east


def godunov(left, right):
    rho_l, p_l, u_l, s_l, t_l = left
    rho_r, p_r, u_r, s_r, t_r = right
    inv_l = lax.rsqrt(GAMMA * (p_l * rho_l))
    inv_r = lax.rsqrt(GAMMA * (p_r * rho_r))
    jump = u_r - u_l
    floor = STAR_FRAC * jnp.minimum(p_l, p_r)
    star = (inv_l * p_l + inv_r * p_r - jump) / (inv_l + inv_r)
    star = jnp.maximum(star, floor)
    slope_l = RATIO_G / p_l
    slope_r = RATIO_G / p_r

    def side(star, p, inv, slope):
        root = lax.rsqrt((1.0 - RATIO_G) + slope * star)
        scaled = inv * root
        return root, scaled, (star - p) * scaled

    for _ in range(RIEMANN_ITERS):
        root_l, scaled_l, f_l = side(star, p_l, inv_l, slope_l)
        root_r, scaled_r, f_r = side(star, p_r, inv_r, slope_r)
        twice = scaled_l * (1.0 + root_l * root_l) + scaled_r * (1.0 + root_r * root_r)
        star = star - 2.0 * (jump + f_l + f_r) / twice
        star = jnp.maximum(star, floor)
    _, _, f_l = side(star, p_l, inv_l, slope_l)
    _, _, f_r = side(star, p_r, inv_r, slope_r)
    speed = 0.5 * ((u_l - f_l) + (u_r + f_r))
    upwind = speed > 0.0
    rho = jnp.where(upwind, rho_l, rho_r)
    p = jnp.where(upwind, p_l, p_r)
    s = jnp.where(upwind, s_l, s_r)
    t = jnp.where(upwind, t_l, t_r)
    mass = rho * speed
    energy = p * (1.0 / (GAMMA - 1.0)) + 0.5 * rho * (speed * speed + s * s + t * t)
    return (mass, (energy + star) * speed, mass * speed + star, mass * s, mass * t)


def wall_flux(state, sign):
    rho, p, u, s, t = state
    inv = lax.rsqrt(GAMMA * (p * rho))
    image = sign * u
    jump = image - u
    floor = STAR_FRAC * p
    star = jnp.maximum(p - 0.5 * jump / inv, floor)
    slope = RATIO_G / p
    for _ in range(RIEMANN_ITERS):
        root = lax.rsqrt((1.0 - RATIO_G) + slope * star)
        scaled = inv * root
        twice_f = 2.0 * (star - p) * scaled
        star = jnp.maximum(star - (jump + twice_f) / (scaled * (1.0 + root * root)), floor)
    speed = 0.5 * (u + image)
    mass = rho * speed
    energy = p * (1.0 / (GAMMA - 1.0)) + 0.5 * rho * (speed * speed + s * s + t * t)
    return (mass, (energy + star) * speed, mass * speed + star, mass * s, mass * t)


def advance(cell, flux_low, flux_high):
    rho, p, u, s, t = cell
    change = [COURANT * (high - low) for low, high in zip(flux_low, flux_high)]
    mass = rho - change[0]
    energy = p * (1.0 / (GAMMA - 1.0)) + 0.5 * rho * (u * u + s * s + t * t) - change[1]
    mom = [rho * v - c for v, c in zip((u, s, t), change[2:])]
    rho = jnp.maximum(mass, DENS_FLOOR)
    inv = 1.0 / rho
    u, s, t = (m * inv for m in mom)
    p = (GAMMA - 1.0) * (energy - 0.5 * rho * (u * u + s * s + t * t))
    return rho, jnp.maximum(p, PRESS_FLOOR), u, s, t


def field_order(normal):
    return (0, 1, normal) + tuple(v for v in (2, 3, 4) if v != normal)


def sign_of(flag):
    return jnp.where(flag == 1, -1.0, 1.0).astype(jnp.float32)


def x_kernel(
    bounds, dens, press, vel, main, first, second, held, flags, sems, left, right, last, turn
):
    planes, rows, cells = dens.shape
    copies = [pltpu.make_async_copy(bounds, flags, sems.at[5])]
    for f, source in enumerate((dens, press, vel.at[0], vel.at[1], vel.at[2])):
        copies.append(pltpu.make_async_copy(source, held.at[f], sems.at[f]))
    for copy in copies:
        copy.start()
    for copy in copies:
        copy.wait()
    pair = 2
    half = cells // LANES
    lane = lax.broadcasted_iota(jnp.int32, (pair * rows, cells), 1)
    end = lax.broadcasted_iota(jnp.int32, (pair * rows, LANES), 1) == LANES - 1
    sign_low, sign_high = sign_of(flags[0]), sign_of(flags[1])

    def load(field, start):
        return held[field, start : start + pair].reshape(pair * rows, cells)

    for start in range(0, planes, pair):
        block = slice(start * rows, (start + pair) * rows)
        for field in range(5):
            low = sign_low if field == 2 else 1.0
            high = sign_high if field == 2 else 1.0
            cell = load(field, start)
            before = jnp.where(lane == 0, low * cell, pltpu.roll(cell, 1, 1))
            after = jnp.where(lane == cells - 1, high * cell, pltpu.roll(cell, cells - 1, 1))
            face = face_value(pltpu.roll(before, 1, 1), before, cell, after)
            face = jnp.where(lane == 0, 0.5 * (before + cell), face)
            face_next = jnp.where(
                lane == cells - 1, 0.5 * (cell + after), pltpu.roll(face, cells - 1, 1)
            )
            west, east = cell_edges(cell, face, face_next)
            left[field, block, :] = jnp.where(lane == 0, low * west, pltpu.roll(east, 1, 1))
            right[field, block, :] = west
            last[field, block, :] = east[:, cells - LANES :]

    for start in range(0, planes, pair):
        block = slice(start * rows, (start + pair) * rows)
        flux = godunov(
            [left[f, block, :] for f in range(5)], [right[f, block, :] for f in range(5)]
        )
        upper = wall_flux([last[f, block, :] for f in range(5)], sign_high)
        after = []
        for f in range(5):
            rolled = pltpu.roll(flux[f], cells - 1, 1)
            tail = jnp.where(end, upper[f], rolled[:, cells - LANES :])
            after.append(jnp.concatenate([rolled[:, : cells - LANES], tail], axis=1))
        new = advance([load(f, start) for f in range(5)], flux, after)
        for f in range(5):
            for h in range(half):
                base = ((f * half + h) * planes + start) * rows
                turn[base : base + pair * rows, :] = new[f][:, h * LANES : (h + 1) * LANES]
    turn_over(turn, main, half)
    edge_blocks("row", main, first, second)


def turn_over(turn, main, half):
    fields, outer, inner, _ = main.shape
    for f in range(fields):
        for h in range(half):
            base = (f * half + h) * outer * inner
            for j in range(outer):
                main[f, j, :, h * LANES : (h + 1) * LANES] = turn[pl.ds(base + j, inner, stride=outer), :]


RING = 4
ROW_LATE = (3, 7)


def ring_in(rings):
    ring = lax.axis_index("gz") // RING
    return functools.reduce(jnp.logical_or, [ring == k for k in rings], ring < 0)


def upper_first(axis):
    if axis == "gz":
        return lax.rem(lax.axis_index("gz"), 2) == 0
    return lax.rem(lax.axis_index("row"), 2) == jnp.where(ring_in(ROW_LATE), 0, 1)


def edge_blocks(axis, main, first, second):
    outer = main.shape[1]
    upper = upper_first(axis)
    start_first = jnp.where(upper, outer - WIDTH, 0)
    start_second = jnp.where(upper, 0, outer - WIDTH)
    for f in range(5):
        for k in range(WIDTH):
            first[f, k] = main[f, start_first + k]
            second[f, k] = main[f, start_second + k]


def sweep_outer(axis, faces, bounds, flags, normal, main, first, second, ghost, left, right, flux, store):
    outer, rows, cells = main.shape[1:]
    half = cells // LANES
    place, count = lax.axis_index(axis), lax.axis_size(axis)
    upper = upper_first(axis)

    @pl.when(upper)
    def _():
        ghost[:, :WIDTH] = second[...]
        ghost[:, WIDTH:] = first[...]

    @pl.when(jnp.logical_not(upper))
    def _():
        ghost[:, :WIDTH] = first[...]
        ghost[:, WIDTH:] = second[...]

    def wall(slot, edge, step, flag):
        for f in range(5):
            sign = sign_of(flag) if f == normal else 1.0
            for k in range(WIDTH):
                ghost[f, slot(k)] = jnp.where(flag == 1, sign * main[f, edge + step * k], main[f, edge])

    @pl.when(place == 0)
    def _():
        pltpu.sync_copy(bounds, flags)
        wall(lambda k: WIDTH - 1 - k, 0, 1, flags[faces])

    @pl.when(place == count - 1)
    def _():
        pltpu.sync_copy(bounds, flags)
        wall(lambda k: WIDTH + k, outer - 1, -1, flags[faces + 1])

    order = field_order(normal)
    for f in range(5):
        for h in range(half):
            part = slice(h * LANES, (h + 1) * LANES)

            def cell(i):
                if i < 0:
                    return ghost[f, WIDTH + i, :, part]
                if i >= outer:
                    return ghost[f, WIDTH + i - outer, :, part]
                return main[f, i, :, part]

            value = {i: cell(i) for i in range(-WIDTH, outer + WIDTH)}
            face = None
            for i in range(-1, outer + 1):
                if face is None:
                    face = face_value(*(value[i + d] for d in (-2, -1, 0, 1)))
                face_next = face_value(*(value[i + d] for d in (-1, 0, 1, 2)))
                west, east = cell_edges(value[i], face, face_next)
                if i < outer:
                    left[f, i + 1, :, part] = east
                if i >= 0:
                    right[f, i, :, part] = west
                face = face_next
    chunk = 3
    for start in range(0, outer + 1, chunk):
        stop = min(start + chunk, outer + 1)
        for h in range(half):
            part = slice(h * LANES, (h + 1) * LANES)
            out = godunov(
                [left[f, start:stop, :, part] for f in order],
                [right[f, start:stop, :, part] for f in order],
            )
            for f in range(5):
                flux[f, start:stop, :, part] = out[f]
    for i in range(outer):
        new = advance(
            [main[f, i] for f in order], [flux[f, i] for f in range(5)], [flux[f, i + 1] for f in range(5)]
        )
        store(i, {f: new[k] for k, f in enumerate(order)})


def y_kernel(bounds, main, first, second, out, out_first, out_second, flags, ghost, left, right, flux, turn):
    outer, rows, cells = main.shape[1:]
    half = cells // LANES

    def store(i, new):
        for f in range(5):
            for h in range(half):
                base = ((f * half + h) * outer + i) * rows
                turn[base : base + rows, :] = new[f][:, h * LANES : (h + 1) * LANES]

    sweep_outer("row", 2, bounds, flags, 3, main, first, second, ghost, left, right, flux, store)
    turn_over(turn, out, half)
    edge_blocks("gz", out, out_first, out_second)


def z_kernel(bounds, main, first, second, dens, press, vel, flags, ghost, left, right, flux):
    def store(i, new):
        dens[i] = new[0]
        press[i] = new[1]
        for v in range(3):
            vel[v, i] = new[2 + v]

    sweep_outer("gz", 4, bounds, flags, 4, main, first, second, ghost, left, right, flux, store)


def swap(block, places):
    rows = lax.axis_size("row")
    pairs = []
    for (g, r), (h, q) in places:
        pairs += [(g * rows + r, h * rows + q), (h * rows + q, g * rows + r)]
    return lax.ppermute(block, ("gz", "row"), pairs)


def row_swap(block, turn):
    places = []
    for g in range(lax.axis_size("gz")):
        start = turn if g // RING in ROW_LATE else 1 - turn
        places += [((g, r), (g, r + 1)) for r in range(start, lax.axis_size("row") - 1, 2)]
    return swap(block, places)


def gz_swap(block, turn):
    places = [
        ((g, r), (g + 1, r))
        for g in range(turn, lax.axis_size("gz") - 1, 2)
        for r in range(lax.axis_size("row"))
    ]
    return swap(block, places)


def on_device(density, pressure, velocity, boundary):
    planes, rows, cells = density.shape
    half = cells // LANES
    f32 = jnp.float32
    hbm = pl.BlockSpec(memory_space=pltpu.HBM)
    flags = pltpu.SMEM((6,), jnp.int32)
    vmem = pl.BlockSpec(memory_space=pltpu.VMEM)
    params = pltpu.CompilerParams(vmem_limit_bytes=32 << 20)
    by_y = jax.ShapeDtypeStruct((5, rows, planes, cells), f32)
    by_z = jax.ShapeDtypeStruct((5, planes, rows, cells), f32)
    y_edge = jax.ShapeDtypeStruct((5, WIDTH, planes, cells), f32)
    z_edge = jax.ShapeDtypeStruct((5, WIDTH, rows, cells), f32)
    turn = pltpu.VMEM((5 * half * planes * rows, LANES), f32)

    def work(outer, inner):
        return [
            flags,
            pltpu.VMEM((5, 2 * WIDTH, inner, cells), f32),
            pltpu.VMEM((5, outer + 1, inner, cells), f32),
            pltpu.VMEM((5, outer + 1, inner, cells), f32),
            pltpu.VMEM((5, outer + 1, inner, cells), f32),
        ]

    main, first, second = pl.pallas_call(
        x_kernel,
        out_shape=(by_y, y_edge, y_edge),
        in_specs=[hbm, hbm, hbm, hbm],
        out_specs=(vmem, vmem, vmem),
        scratch_shapes=[
            pltpu.VMEM((5, planes, rows, cells), f32),
            flags,
            pltpu.SemaphoreType.DMA((6,)),
            pltpu.VMEM((5, planes * rows, cells), f32),
            pltpu.VMEM((5, planes * rows, cells), f32),
            pltpu.VMEM((5, planes * rows, LANES), f32),
            turn,
        ],
        compiler_params=params,
        name="x_sweep",
    )(*(pltpu.with_memory_space_constraint(a, pltpu.HBM) for a in (boundary, density, pressure, velocity)))
    first = row_swap(first, 0)
    second = row_swap(second, 1)
    main, first, second = pl.pallas_call(
        y_kernel,
        out_shape=(by_z, z_edge, z_edge),
        in_specs=[hbm, vmem, vmem, vmem],
        out_specs=(vmem, vmem, vmem),
        scratch_shapes=work(rows, planes) + [turn],
        compiler_params=params,
        name="y_sweep",
    )(boundary, main, first, second)
    first = gz_swap(first, 0)
    second = gz_swap(second, 1)
    return pl.pallas_call(
        z_kernel,
        out_shape=(
            jax.ShapeDtypeStruct(density.shape, f32),
            jax.ShapeDtypeStruct(pressure.shape, f32),
            jax.ShapeDtypeStruct(velocity.shape, f32),
        ),
        in_specs=[hbm, vmem, vmem, vmem],
        out_specs=(vmem, vmem, vmem),
        scratch_shapes=work(planes, rows),
        compiler_params=params,
        name="z_sweep",
    )(boundary, main, first, second)


def solution(mesh):
    in_specs = (P("gz", "row", None), P("gz", "row", None), P(None, "gz", "row", None), P())
    out_specs = (P("gz", "row", None), P("gz", "row", None), P(None, "gz", "row", None))
    return jax.shard_map(
        on_device, mesh=mesh, in_specs=in_specs, out_specs=out_specs, check_vma=False
    )
```

```python
import functools

import jax
import jax.numpy as jnp
from jax import lax
from jax.experimental import pallas as pl
from jax.experimental.pallas import tpu as pltpu
from jax.sharding import PartitionSpec as P

RIEMANN_ITERS = 4
GAMMA = 1.4
COURANT = 0.05
DENS_FLOOR = 0.02
PRESS_FLOOR = 0.02
STAR_FRAC = 0.1
RATIO_G = (GAMMA + 1.0) / (2.0 * GAMMA)
WIDTH = 3
LANES = 128


def face_value(far_left, left, right, far_right):
    value = (7.0 / 12.0) * (left + right) - (1.0 / 12.0) * (far_left + far_right)
    return jnp.clip(value, jnp.minimum(left, right), jnp.maximum(left, right))


def cell_edges(cell, face_left, face_right):
    to_left = face_left - cell
    to_right = face_right - cell
    two_left = 2.0 * jnp.abs(to_left)
    two_right = 2.0 * jnp.abs(to_right)
    west = cell + jnp.clip(to_left, -two_right, two_right)
    east = cell + jnp.clip(to_right, -two_left, two_left)
    return west, east


def godunov(left, right):
    rho_l, p_l, u_l, s_l, t_l = left
    rho_r, p_r, u_r, s_r, t_r = right
    inv_l = lax.rsqrt(GAMMA * (p_l * rho_l))
    inv_r = lax.rsqrt(GAMMA * (p_r * rho_r))
    jump = u_r - u_l
    floor = STAR_FRAC * jnp.minimum(p_l, p_r)
    star = (inv_l * p_l + inv_r * p_r - jump) / (inv_l + inv_r)
    star = jnp.maximum(star, floor)
    slope_l = RATIO_G / p_l
    slope_r = RATIO_G / p_r

    def side(star, p, inv, slope):
        root = lax.rsqrt((1.0 - RATIO_G) + slope * star)
        scaled = inv * root
        return root, scaled, (star - p) * scaled

    for _ in range(RIEMANN_ITERS):
        root_l, scaled_l, f_l = side(star, p_l, inv_l, slope_l)
        root_r, scaled_r, f_r = side(star, p_r, inv_r, slope_r)
        twice = scaled_l * (1.0 + root_l * root_l) + scaled_r * (1.0 + root_r * root_r)
        star = star - 2.0 * (jump + f_l + f_r) / twice
        star = jnp.maximum(star, floor)
    _, _, f_l = side(star, p_l, inv_l, slope_l)
    _, _, f_r = side(star, p_r, inv_r, slope_r)
    speed = 0.5 * ((u_l - f_l) + (u_r + f_r))
    upwind = speed > 0.0
    rho = jnp.where(upwind, rho_l, rho_r)
    p = jnp.where(upwind, p_l, p_r)
    s = jnp.where(upwind, s_l, s_r)
    t = jnp.where(upwind, t_l, t_r)
    mass = rho * speed
    energy = p * (1.0 / (GAMMA - 1.0)) + 0.5 * rho * (speed * speed + s * s + t * t)
    return (mass, (energy + star) * speed, mass * speed + star, mass * s, mass * t)


def wall_flux(state, sign):
    rho, p, u, s, t = state
    inv = lax.rsqrt(GAMMA * (p * rho))
    image = sign * u
    jump = image - u
    floor = STAR_FRAC * p
    star = jnp.maximum(p - 0.5 * jump / inv, floor)
    slope = RATIO_G / p
    for _ in range(RIEMANN_ITERS):
        root = lax.rsqrt((1.0 - RATIO_G) + slope * star)
        scaled = inv * root
        twice_f = 2.0 * (star - p) * scaled
        star = jnp.maximum(star - (jump + twice_f) / (scaled * (1.0 + root * root)), floor)
    speed = 0.5 * (u + image)
    mass = rho * speed
    energy = p * (1.0 / (GAMMA - 1.0)) + 0.5 * rho * (speed * speed + s * s + t * t)
    return (mass, (energy + star) * speed, mass * speed + star, mass * s, mass * t)


def advance(cell, flux_low, flux_high):
    rho, p, u, s, t = cell
    change = [COURANT * (high - low) for low, high in zip(flux_low, flux_high)]
    mass = rho - change[0]
    energy = p * (1.0 / (GAMMA - 1.0)) + 0.5 * rho * (u * u + s * s + t * t) - change[1]
    mom = [rho * v - c for v, c in zip((u, s, t), change[2:])]
    rho = jnp.maximum(mass, DENS_FLOOR)
    inv = 1.0 / rho
    u, s, t = (m * inv for m in mom)
    p = (GAMMA - 1.0) * (energy - 0.5 * rho * (u * u + s * s + t * t))
    return rho, jnp.maximum(p, PRESS_FLOOR), u, s, t


def field_order(normal):
    return (0, 1, normal) + tuple(v for v in (2, 3, 4) if v != normal)


def sign_of(flag):
    return jnp.where(flag == 1, -1.0, 1.0).astype(jnp.float32)


def x_kernel(
    bounds, dens, press, vel, main, first, second, held, flags, sems, left, right, last, turn
):
    planes, rows, cells = dens.shape
    copies = [pltpu.make_async_copy(bounds, flags, sems.at[5])]
    for f, source in enumerate((dens, press, vel.at[0], vel.at[1], vel.at[2])):
        copies.append(pltpu.make_async_copy(source, held.at[f], sems.at[f]))
    for copy in copies:
        copy.start()
    for copy in copies:
        copy.wait()
    pair = 4
    half = cells // LANES
    lane = lax.broadcasted_iota(jnp.int32, (pair * rows, cells), 1)
    end = lax.broadcasted_iota(jnp.int32, (pair * rows, LANES), 1) == LANES - 1
    sign_low, sign_high = sign_of(flags[0]), sign_of(flags[1])

    def load(field, start):
        return held[field, start : start + pair].reshape(pair * rows, cells)

    for start in range(0, planes, pair):
        block = slice(start * rows, (start + pair) * rows)
        for field in range(5):
            low = sign_low if field == 2 else 1.0
            high = sign_high if field == 2 else 1.0
            cell = load(field, start)
            before = jnp.where(lane == 0, low * cell, pltpu.roll(cell, 1, 1))
            after = jnp.where(lane == cells - 1, high * cell, pltpu.roll(cell, cells - 1, 1))
            face = face_value(pltpu.roll(before, 1, 1), before, cell, after)
            face = jnp.where(lane == 0, 0.5 * (before + cell), face)
            face_next = jnp.where(
                lane == cells - 1, 0.5 * (cell + after), pltpu.roll(face, cells - 1, 1)
            )
            west, east = cell_edges(cell, face, face_next)
            left[field, block, :] = jnp.where(lane == 0, low * west, pltpu.roll(east, 1, 1))
            right[field, block, :] = west
            last[field, block, :] = east[:, cells - LANES :]

    for start in range(0, planes, pair):
        block = slice(start * rows, (start + pair) * rows)
        flux = godunov(
            [left[f, block, :] for f in range(5)], [right[f, block, :] for f in range(5)]
        )
        upper = wall_flux([last[f, block, :] for f in range(5)], sign_high)
        after = []
        for f in range(5):
            rolled = pltpu.roll(flux[f], cells - 1, 1)
            tail = jnp.where(end, upper[f], rolled[:, cells - LANES :])
            after.append(jnp.concatenate([rolled[:, : cells - LANES], tail], axis=1))
        new = advance([load(f, start) for f in range(5)], flux, after)
        for f in range(5):
            for h in range(half):
                base = ((f * half + h) * planes + start) * rows
                turn[base : base + pair * rows, :] = new[f][:, h * LANES : (h + 1) * LANES]
    turn_over(turn, main, half)
    edge_blocks("row", main, first, second)


def turn_over(turn, main, half):
    fields, outer, inner, _ = main.shape
    for f in range(fields):
        for h in range(half):
            base = (f * half + h) * outer * inner
            for j in range(outer):
                main[f, j, :, h * LANES : (h + 1) * LANES] = turn[pl.ds(base + j, inner, stride=outer), :]


RING = 4
ROW_LATE = (3, 7)


def ring_in(rings):
    ring = lax.axis_index("gz") // RING
    return functools.reduce(jnp.logical_or, [ring == k for k in rings], ring < 0)


def parity(axis):
    return lax.rem(lax.axis_index(axis), 2)


def upper_first(axis):
    if axis == "gz":
        return lax.rem(lax.axis_index("gz"), 2) == 0
    return lax.rem(lax.axis_index("row"), 2) == jnp.where(ring_in(ROW_LATE), 0, 1)


def edge_blocks(axis, main, first, second):
    outer = main.shape[1]
    upper = upper_first(axis)
    start_first = jnp.where(upper, outer - WIDTH, 0)
    start_second = jnp.where(upper, 0, outer - WIDTH)
    for f in range(5):
        for k in range(WIDTH):
            first[f, k] = main[f, start_first + k]
            second[f, k] = main[f, start_second + k]


def sweep_outer(axis, faces, bounds, flags, normal, main, first, second, ghost, left, right, flux, store):
    outer, rows, cells = main.shape[1:]
    half = cells // LANES
    place, count = lax.axis_index(axis), lax.axis_size(axis)
    upper = upper_first(axis)

    @pl.when(upper)
    def _():
        ghost[:, :WIDTH] = second[...]
        ghost[:, WIDTH:] = first[...]

    @pl.when(jnp.logical_not(upper))
    def _():
        ghost[:, :WIDTH] = first[...]
        ghost[:, WIDTH:] = second[...]

    def wall(slot, edge, step, flag):
        for f in range(5):
            sign = sign_of(flag) if f == normal else 1.0
            for k in range(WIDTH):
                ghost[f, slot(k)] = jnp.where(flag == 1, sign * main[f, edge + step * k], main[f, edge])

    @pl.when(place == 0)
    def _():
        pltpu.sync_copy(bounds, flags)
        wall(lambda k: WIDTH - 1 - k, 0, 1, flags[faces])

    @pl.when(place == count - 1)
    def _():
        pltpu.sync_copy(bounds, flags)
        wall(lambda k: WIDTH + k, outer - 1, -1, flags[faces + 1])

    order = field_order(normal)
    for f in range(5):
        for h in range(half):
            part = slice(h * LANES, (h + 1) * LANES)

            def cell(i):
                if i < 0:
                    return ghost[f, WIDTH + i, :, part]
                if i >= outer:
                    return ghost[f, WIDTH + i - outer, :, part]
                return main[f, i, :, part]

            value = {i: cell(i) for i in range(-WIDTH, outer + WIDTH)}
            face = None
            for i in range(-1, outer + 1):
                if face is None:
                    face = face_value(*(value[i + d] for d in (-2, -1, 0, 1)))
                face_next = face_value(*(value[i + d] for d in (-1, 0, 1, 2)))
                west, east = cell_edges(value[i], face, face_next)
                if i < outer:
                    left[f, i + 1, :, part] = east
                if i >= 0:
                    right[f, i, :, part] = west
                face = face_next
    chunk = 3
    for start in range(0, outer + 1, chunk):
        stop = min(start + chunk, outer + 1)
        for h in range(half):
            part = slice(h * LANES, (h + 1) * LANES)
            out = godunov(
                [left[f, start:stop, :, part] for f in order],
                [right[f, start:stop, :, part] for f in order],
            )
            for f in range(5):
                flux[f, start:stop, :, part] = out[f]
    for i in range(outer):
        new = advance(
            [main[f, i] for f in order], [flux[f, i] for f in range(5)], [flux[f, i + 1] for f in range(5)]
        )
        store(i, {f: new[k] for k, f in enumerate(order)})


def y_kernel(bounds, main, first, second, out, out_first, out_second, flags, ghost, left, right, flux, turn):
    outer, rows, cells = main.shape[1:]
    half = cells // LANES

    def store(i, new):
        for f in range(5):
            for h in range(half):
                base = ((f * half + h) * outer + i) * rows
                turn[base : base + rows, :] = new[f][:, h * LANES : (h + 1) * LANES]

    sweep_outer("row", 2, bounds, flags, 3, main, first, second, ghost, left, right, flux, store)
    turn_over(turn, out, half)
    edge_blocks("gz", out, out_first, out_second)


def part_faces(block, count, flux, shift, left, right, order):
    cells = block.shape[-1]
    for f in range(5):
        for h in range(cells // LANES):
            part = slice(h * LANES, (h + 1) * LANES)
            value = [block[f, i, :, part] for i in range(count + 5)]
            face = face_value(*value[:4])
            for i in range(2, count + 3):
                face_next = face_value(*value[i - 1 : i + 3])
                west, east = cell_edges(value[i], face, face_next)
                if i < count + 2:
                    left[f, i - 2, :, part] = east
                if i > 2:
                    right[f, i - 3, :, part] = west
                face = face_next
    for start in range(0, count, WIDTH):
        for h in range(cells // LANES):
            part = slice(h * LANES, (h + 1) * LANES)
            out = godunov(
                [left[f, start : start + WIDTH, :, part] for f in order],
                [right[f, start : start + WIDTH, :, part] for f in order],
            )
            for f in range(5):
                flux[f, pl.ds(start + shift, WIDTH), :, part] = out[f]


def part_cells(block, skip, count, flux, held, order):
    for i in range(count):
        new = advance(
            [block[f, skip + i] for f in order], [flux[f, i] for f in range(5)], [flux[f, i + 1] for f in range(5)]
        )
        for k, f in enumerate(order):
            held[f, i] = new[k]


def leave(held, dens, press, vel, base, sems):
    count = held.shape[1]
    part = pl.ds(base, count)
    copies = [
        pltpu.make_async_copy(held.at[0], dens.at[part], sems.at[0]),
        pltpu.make_async_copy(held.at[1], press.at[part], sems.at[1]),
    ]
    for v in range(3):
        copies.append(pltpu.make_async_copy(held.at[2 + v], vel.at[v, part], sems.at[2 + v]))
    for copy in copies:
        copy.start()
    for copy in copies:
        copy.wait()


def z_most_kernel(main, first, dens, press, vel, border, block, left, right, flux, held, sems):
    outer = main.shape[1]
    upper = parity("gz") == 0
    order = field_order(4)
    most = outer - WIDTH
    block[:, pl.ds(jnp.where(upper, 0, WIDTH), outer)] = main[...]
    block[:, pl.ds(jnp.where(upper, outer, 0), WIDTH)] = first[...]
    part_faces(block, most + 1, flux, 0, left, right, order)
    border[...] = flux[:, jnp.where(upper, 0, most)]
    part_cells(block, WIDTH, most, flux, held, order)
    leave(held, dens, press, vel, jnp.where(upper, WIDTH, 0), sems)


def z_rest_kernel(
    bounds, main, second, border, dens_in, press_in, vel_in, dens, press, vel, flags, block, left, right, flux, held, sems
):
    del dens_in, press_in, vel_in
    outer = main.shape[1]
    place, count = lax.axis_index("gz"), lax.axis_size("gz")
    upper = lax.rem(place, 2) == 0
    order = field_order(4)
    near = outer - WIDTH
    block[:, pl.ds(jnp.where(upper, WIDTH, 0), near)] = main[:, pl.ds(jnp.where(upper, 0, WIDTH), near)]
    block[:, pl.ds(jnp.where(upper, 0, near), WIDTH)] = second[...]

    def wall(slot, edge, step, flag):
        for f in range(5):
            sign = sign_of(flag) if f == 4 else 1.0
            for k in range(WIDTH):
                block[f, slot(k)] = jnp.where(flag == 1, sign * main[f, edge + step * k], main[f, edge])

    @pl.when(place == 0)
    def _():
        pltpu.sync_copy(bounds, flags)
        wall(lambda k: WIDTH - 1 - k, 0, 1, flags[4])

    @pl.when(place == count - 1)
    def _():
        pltpu.sync_copy(bounds, flags)
        wall(lambda k: near + k, outer - 1, -1, flags[5])

    part_faces(block, WIDTH, flux, jnp.where(upper, 0, 1), left, right, order)
    flux[:, jnp.where(upper, WIDTH, 0)] = border[...]
    part_cells(block, jnp.where(upper, WIDTH, WIDTH - 1), WIDTH, flux, held, order)
    leave(held, dens, press, vel, jnp.where(upper, 0, near), sems)


def swap(block, places):
    rows = lax.axis_size("row")
    pairs = []
    for (g, r), (h, q) in places:
        pairs += [(g * rows + r, h * rows + q), (h * rows + q, g * rows + r)]
    return lax.ppermute(block, ("gz", "row"), pairs)


def row_swap(block, turn):
    places = []
    for g in range(lax.axis_size("gz")):
        start = turn if g // RING in ROW_LATE else 1 - turn
        places += [((g, r), (g, r + 1)) for r in range(start, lax.axis_size("row") - 1, 2)]
    return swap(block, places)


def gz_swap(block, turn):
    places = [
        ((g, r), (g + 1, r))
        for g in range(turn, lax.axis_size("gz") - 1, 2)
        for r in range(lax.axis_size("row"))
    ]
    return swap(block, places)


def on_device(density, pressure, velocity, boundary):
    planes, rows, cells = density.shape
    half = cells // LANES
    f32 = jnp.float32
    hbm = pl.BlockSpec(memory_space=pltpu.HBM)
    flags = pltpu.SMEM((6,), jnp.int32)
    vmem = pl.BlockSpec(memory_space=pltpu.VMEM)
    params = pltpu.CompilerParams(vmem_limit_bytes=32 << 20)
    by_y = jax.ShapeDtypeStruct((5, rows, planes, cells), f32)
    by_z = jax.ShapeDtypeStruct((5, planes, rows, cells), f32)
    y_edge = jax.ShapeDtypeStruct((5, WIDTH, planes, cells), f32)
    z_edge = jax.ShapeDtypeStruct((5, WIDTH, rows, cells), f32)
    turn = pltpu.VMEM((5 * half * planes * rows, LANES), f32)

    def work(outer, inner):
        return [
            flags,
            pltpu.VMEM((5, 2 * WIDTH, inner, cells), f32),
            pltpu.VMEM((5, outer + 1, inner, cells), f32),
            pltpu.VMEM((5, outer + 1, inner, cells), f32),
            pltpu.VMEM((5, outer + 1, inner, cells), f32),
        ]

    main, first, second = pl.pallas_call(
        x_kernel,
        out_shape=(by_y, y_edge, y_edge),
        in_specs=[hbm, hbm, hbm, hbm],
        out_specs=(vmem, vmem, vmem),
        scratch_shapes=[
            pltpu.VMEM((5, planes, rows, cells), f32),
            flags,
            pltpu.SemaphoreType.DMA((6,)),
            pltpu.VMEM((5, planes * rows, cells), f32),
            pltpu.VMEM((5, planes * rows, cells), f32),
            pltpu.VMEM((5, planes * rows, LANES), f32),
            turn,
        ],
        compiler_params=params,
        name="x_sweep",
    )(*(pltpu.with_memory_space_constraint(a, pltpu.HBM) for a in (boundary, density, pressure, velocity)))
    first = row_swap(first, 0)
    second = row_swap(second, 1)
    main, first, second = pl.pallas_call(
        y_kernel,
        out_shape=(by_z, z_edge, z_edge),
        in_specs=[hbm, vmem, vmem, vmem],
        out_specs=(vmem, vmem, vmem),
        scratch_shapes=work(rows, planes) + [turn],
        compiler_params=params,
        name="y_sweep",
    )(boundary, main, first, second)
    first = gz_swap(first, 0)
    second = gz_swap(second, 1)
    results = (
        jax.ShapeDtypeStruct(density.shape, f32),
        jax.ShapeDtypeStruct(pressure.shape, f32),
        jax.ShapeDtypeStruct(velocity.shape, f32),
    )

    def z_work(faces, whole, done):
        return [
            pltpu.VMEM((5, whole, rows, cells), f32),
            pltpu.VMEM((5, faces, rows, cells), f32),
            pltpu.VMEM((5, faces, rows, cells), f32),
            pltpu.VMEM((5, done + 1, rows, cells), f32),
            pltpu.VMEM((5, done, rows, cells), f32),
            pltpu.SemaphoreType.DMA((5,)),
        ]

    most = planes - WIDTH
    *partial, border = pl.pallas_call(
        z_most_kernel,
        out_shape=results + (jax.ShapeDtypeStruct((5, rows, cells), f32),),
        in_specs=[vmem, vmem],
        out_specs=(hbm, hbm, hbm, vmem),
        scratch_shapes=z_work(most + 1, planes + WIDTH, most),
        compiler_params=params,
        name="z_sweep_most",
    )(main, first)
    return pl.pallas_call(
        z_rest_kernel,
        out_shape=results,
        in_specs=[hbm, vmem, vmem, vmem, hbm, hbm, hbm],
        out_specs=(hbm, hbm, hbm),
        scratch_shapes=[flags] + z_work(WIDTH, planes, WIDTH),
        input_output_aliases={4: 0, 5: 1, 6: 2},
        compiler_params=params,
        name="z_sweep_rest",
    )(boundary, main, second, border, *partial)


def solution(mesh):
    in_specs = (P("gz", "row", None), P("gz", "row", None), P(None, "gz", "row", None), P())
    out_specs = (P("gz", "row", None), P("gz", "row", None), P(None, "gz", "row", None))
    return jax.shard_map(
        on_device, mesh=mesh, in_specs=in_specs, out_specs=out_specs, check_vma=False
    )
```

```python
import functools

import jax
import jax.numpy as jnp
from jax import lax
from jax.experimental import pallas as pl
from jax.experimental.pallas import tpu as pltpu
from jax.sharding import PartitionSpec as P

RIEMANN_ITERS = 4
GAMMA = 1.4
COURANT = 0.05
DENS_FLOOR = 0.02
PRESS_FLOOR = 0.02
STAR_FRAC = 0.1
RATIO_G = (GAMMA + 1.0) / (2.0 * GAMMA)
WIDTH = 3
LANES = 128


def face_value(far_left, left, right, far_right):
    value = (7.0 / 12.0) * (left + right) - (1.0 / 12.0) * (far_left + far_right)
    return jnp.clip(value, jnp.minimum(left, right), jnp.maximum(left, right))


def cell_edges(cell, face_left, face_right):
    to_left = face_left - cell
    to_right = face_right - cell
    two_left = 2.0 * jnp.abs(to_left)
    two_right = 2.0 * jnp.abs(to_right)
    west = cell + jnp.clip(to_left, -two_right, two_right)
    east = cell + jnp.clip(to_right, -two_left, two_left)
    return west, east


def godunov(left, right):
    rho_l, p_l, u_l, s_l, t_l = left
    rho_r, p_r, u_r, s_r, t_r = right
    inv_l = lax.rsqrt(GAMMA * (p_l * rho_l))
    inv_r = lax.rsqrt(GAMMA * (p_r * rho_r))
    jump = u_r - u_l
    floor = STAR_FRAC * jnp.minimum(p_l, p_r)
    star = (inv_l * p_l + inv_r * p_r - jump) / (inv_l + inv_r)
    star = jnp.maximum(star, floor)
    slope_l = RATIO_G / p_l
    slope_r = RATIO_G / p_r

    def side(star, p, inv, slope):
        root = lax.rsqrt((1.0 - RATIO_G) + slope * star)
        scaled = inv * root
        return root, scaled, (star - p) * scaled

    for _ in range(RIEMANN_ITERS):
        root_l, scaled_l, f_l = side(star, p_l, inv_l, slope_l)
        root_r, scaled_r, f_r = side(star, p_r, inv_r, slope_r)
        twice = scaled_l * (1.0 + root_l * root_l) + scaled_r * (1.0 + root_r * root_r)
        star = star - 2.0 * (jump + f_l + f_r) / twice
        star = jnp.maximum(star, floor)
    _, _, f_l = side(star, p_l, inv_l, slope_l)
    _, _, f_r = side(star, p_r, inv_r, slope_r)
    speed = 0.5 * ((u_l - f_l) + (u_r + f_r))
    upwind = speed > 0.0
    rho = jnp.where(upwind, rho_l, rho_r)
    p = jnp.where(upwind, p_l, p_r)
    s = jnp.where(upwind, s_l, s_r)
    t = jnp.where(upwind, t_l, t_r)
    mass = rho * speed
    energy = p * (1.0 / (GAMMA - 1.0)) + 0.5 * rho * (speed * speed + s * s + t * t)
    return (mass, (energy + star) * speed, mass * speed + star, mass * s, mass * t)


def wall_flux(state, sign):
    rho, p, u, s, t = state
    inv = lax.rsqrt(GAMMA * (p * rho))
    image = sign * u
    jump = image - u
    floor = STAR_FRAC * p
    star = jnp.maximum(p - 0.5 * jump / inv, floor)
    slope = RATIO_G / p
    for _ in range(RIEMANN_ITERS):
        root = lax.rsqrt((1.0 - RATIO_G) + slope * star)
        scaled = inv * root
        twice_f = 2.0 * (star - p) * scaled
        star = jnp.maximum(star - (jump + twice_f) / (scaled * (1.0 + root * root)), floor)
    speed = 0.5 * (u + image)
    mass = rho * speed
    energy = p * (1.0 / (GAMMA - 1.0)) + 0.5 * rho * (speed * speed + s * s + t * t)
    return (mass, (energy + star) * speed, mass * speed + star, mass * s, mass * t)


def advance(cell, flux_low, flux_high):
    rho, p, u, s, t = cell
    change = [COURANT * (high - low) for low, high in zip(flux_low, flux_high)]
    mass = rho - change[0]
    energy = p * (1.0 / (GAMMA - 1.0)) + 0.5 * rho * (u * u + s * s + t * t) - change[1]
    mom = [rho * v - c for v, c in zip((u, s, t), change[2:])]
    rho = jnp.maximum(mass, DENS_FLOOR)
    inv = 1.0 / rho
    u, s, t = (m * inv for m in mom)
    p = (GAMMA - 1.0) * (energy - 0.5 * rho * (u * u + s * s + t * t))
    return rho, jnp.maximum(p, PRESS_FLOOR), u, s, t


def field_order(normal):
    return (0, 1, normal) + tuple(v for v in (2, 3, 4) if v != normal)


def sign_of(flag):
    return jnp.where(flag == 1, -1.0, 1.0).astype(jnp.float32)


def x_kernel(
    bounds, dens, press, vel, main, first, second, held, flags, sems, left, right, last, turn
):
    planes, rows, cells = dens.shape
    copies = [pltpu.make_async_copy(bounds, flags, sems.at[5])]
    for f, source in enumerate((dens, press, vel.at[0], vel.at[1], vel.at[2])):
        copies.append(pltpu.make_async_copy(source, held.at[f], sems.at[f]))
    for copy in copies:
        copy.start()
    for copy in copies:
        copy.wait()
    pair = 4
    half = cells // LANES
    lane = lax.broadcasted_iota(jnp.int32, (pair * rows, cells), 1)
    end = lax.broadcasted_iota(jnp.int32, (pair * rows, LANES), 1) == LANES - 1
    sign_low, sign_high = sign_of(flags[0]), sign_of(flags[1])

    def load(field, start):
        return held[field, start : start + pair].reshape(pair * rows, cells)

    for start in range(0, planes, pair):
        block = slice(start * rows, (start + pair) * rows)
        for field in range(5):
            low = sign_low if field == 2 else 1.0
            high = sign_high if field == 2 else 1.0
            cell = load(field, start)
            before = jnp.where(lane == 0, low * cell, pltpu.roll(cell, 1, 1))
            after = jnp.where(lane == cells - 1, high * cell, pltpu.roll(cell, cells - 1, 1))
            face = face_value(pltpu.roll(before, 1, 1), before, cell, after)
            face = jnp.where(lane == 0, 0.5 * (before + cell), face)
            face_next = jnp.where(
                lane == cells - 1, 0.5 * (cell + after), pltpu.roll(face, cells - 1, 1)
            )
            west, east = cell_edges(cell, face, face_next)
            left[field, block, :] = jnp.where(lane == 0, low * west, pltpu.roll(east, 1, 1))
            right[field, block, :] = west
            last[field, block, :] = east[:, cells - LANES :]

    for start in range(0, planes, pair):
        block = slice(start * rows, (start + pair) * rows)
        flux = godunov(
            [left[f, block, :] for f in range(5)], [right[f, block, :] for f in range(5)]
        )
        upper = wall_flux([last[f, block, :] for f in range(5)], sign_high)
        after = []
        for f in range(5):
            rolled = pltpu.roll(flux[f], cells - 1, 1)
            tail = jnp.where(end, upper[f], rolled[:, cells - LANES :])
            after.append(jnp.concatenate([rolled[:, : cells - LANES], tail], axis=1))
        new = advance([load(f, start) for f in range(5)], flux, after)
        for f in range(5):
            for h in range(half):
                base = ((f * half + h) * planes + start) * rows
                turn[base : base + pair * rows, :] = new[f][:, h * LANES : (h + 1) * LANES]
    turn_over(turn, main, half)
    edge_blocks("row", main, first, second)


def turn_over(turn, main, half):
    fields, outer, inner, _ = main.shape
    for f in range(fields):
        for h in range(half):
            base = (f * half + h) * outer * inner
            for j in range(outer):
                main[f, j, :, h * LANES : (h + 1) * LANES] = turn[pl.ds(base + j, inner, stride=outer), :]


RING = 4
ROW_LATE = (3, 7)


def ring_in(rings):
    ring = lax.axis_index("gz") // RING
    return functools.reduce(jnp.logical_or, [ring == k for k in rings], ring < 0)


def parity(axis):
    return lax.rem(lax.axis_index(axis), 2)


def upper_first(axis):
    if axis == "gz":
        return lax.rem(lax.axis_index("gz"), 2) == 0
    return lax.rem(lax.axis_index("row"), 2) == jnp.where(ring_in(ROW_LATE), 0, 1)


def edge_blocks(axis, main, first, second):
    outer = main.shape[1]
    upper = upper_first(axis)
    start_first = jnp.where(upper, outer - WIDTH, 0)
    start_second = jnp.where(upper, 0, outer - WIDTH)
    for f in range(5):
        for k in range(WIDTH):
            first[f, k] = main[f, start_first + k]
            second[f, k] = main[f, start_second + k]


def part_faces(block, count, flux, shift, left, right, order):
    cells = block.shape[-1]
    for f in range(5):
        for h in range(cells // LANES):
            part = slice(h * LANES, (h + 1) * LANES)
            value = [block[f, i, :, part] for i in range(count + 5)]
            face = face_value(*value[:4])
            for i in range(2, count + 3):
                face_next = face_value(*value[i - 1 : i + 3])
                west, east = cell_edges(value[i], face, face_next)
                if i < count + 2:
                    left[f, i - 2, :, part] = east
                if i > 2:
                    right[f, i - 3, :, part] = west
                face = face_next
    for start in range(0, count, WIDTH):
        for h in range(cells // LANES):
            part = slice(h * LANES, (h + 1) * LANES)
            out = godunov(
                [left[f, start : start + WIDTH, :, part] for f in order],
                [right[f, start : start + WIDTH, :, part] for f in order],
            )
            for f in range(5):
                flux[f, pl.ds(start + shift, WIDTH), :, part] = out[f]


def part_cells(block, skip, count, flux, held, order):
    for i in range(count):
        new = advance(
            [block[f, skip + i] for f in order], [flux[f, i] for f in range(5)], [flux[f, i + 1] for f in range(5)]
        )
        for k, f in enumerate(order):
            held[f, i] = new[k]


def leave(held, dens, press, vel, base, sems):
    count = held.shape[1]
    part = pl.ds(base, count)
    copies = [
        pltpu.make_async_copy(held.at[0], dens.at[part], sems.at[0]),
        pltpu.make_async_copy(held.at[1], press.at[part], sems.at[1]),
    ]
    for v in range(3):
        copies.append(pltpu.make_async_copy(held.at[2 + v], vel.at[v, part], sems.at[2 + v]))
    for copy in copies:
        copy.start()
    for copy in copies:
        copy.wait()


def walls(axis, faces, bounds, flags, normal, main, block, upper, low_slot, high_slot):
    outer = main.shape[1]
    place, count = lax.axis_index(axis), lax.axis_size(axis)

    def fill(slot, edge, step, flag):
        for f in range(5):
            sign = sign_of(flag) if f == normal else 1.0
            for k in range(WIDTH):
                block[f, slot(k)] = jnp.where(flag == 1, sign * main[f, edge + step * k], main[f, edge])

    @pl.when(jnp.logical_and(place == 0, jnp.logical_not(upper)))
    def _():
        pltpu.sync_copy(bounds, flags)
        fill(low_slot, 0, 1, flags[faces])

    @pl.when(jnp.logical_and(place == count - 1, upper))
    def _():
        pltpu.sync_copy(bounds, flags)
        fill(high_slot, outer - 1, -1, flags[faces + 1])


def sweep_most(axis, faces, bounds, flags, normal, upper, main, first, border, block, left, right, flux, held):
    outer = main.shape[1]
    order = field_order(normal)
    most = outer - WIDTH
    block[:, pl.ds(jnp.where(upper, 0, WIDTH), outer)] = main[...]
    block[:, pl.ds(jnp.where(upper, outer, 0), WIDTH)] = first[...]
    walls(axis, faces, bounds, flags, normal, main, block, upper, lambda k: WIDTH - 1 - k, lambda k: outer + k)
    part_faces(block, most + 1, flux, 0, left, right, order)
    border[...] = flux[:, jnp.where(upper, 0, most)]
    part_cells(block, WIDTH, most, flux, held, order)


def sweep_rest(axis, faces, bounds, flags, normal, upper, main, second, border, block, left, right, flux, held):
    outer = main.shape[1]
    order = field_order(normal)
    near = outer - WIDTH
    block[:, pl.ds(jnp.where(upper, WIDTH, 0), near)] = main[:, pl.ds(jnp.where(upper, 0, WIDTH), near)]
    block[:, pl.ds(jnp.where(upper, 0, near), WIDTH)] = second[...]
    walls(
        axis, faces, bounds, flags, normal, main, block, jnp.logical_not(upper),
        lambda k: WIDTH - 1 - k, lambda k: near + k,
    )
    part_faces(block, WIDTH, flux, jnp.where(upper, 0, 1), left, right, order)
    flux[:, jnp.where(upper, WIDTH, 0)] = border[...]
    part_cells(block, jnp.where(upper, WIDTH, WIDTH - 1), WIDTH, flux, held, order)


def y_most_kernel(bounds, main, first, held, border, flags, block, left, right, flux):
    sweep_most("row", 2, bounds, flags, 3, upper_first("row"), main, first, border, block, left, right, flux, held)


def y_rest_kernel(
    bounds, main, second, border, done, out, out_first, out_second, flags, block, left, right, flux, held, turn
):
    outer, rows, cells = main.shape[1:]
    half = cells // LANES
    upper = upper_first("row")
    near = outer - WIDTH
    sweep_rest("row", 2, bounds, flags, 3, upper, main, second, border, block, left, right, flux, held)

    def place_rows(source, at):
        count = source.shape[1]
        for f in range(5):
            for h in range(half):
                base = (f * half + h) * outer * rows + at * rows
                for i in range(count):
                    start = pl.multiple_of(base + i * rows, rows)
                    turn[pl.ds(start, rows), :] = source[f, i, :, h * LANES : (h + 1) * LANES]

    place_rows(done, jnp.where(upper, WIDTH, 0))
    place_rows(held, jnp.where(upper, 0, near))
    turn_over(turn, out, half)
    edge_blocks("gz", out, out_first, out_second)


def z_most_kernel(bounds, main, first, dens, press, vel, border, flags, block, left, right, flux, held, sems):
    upper = upper_first("gz")
    sweep_most("gz", 4, bounds, flags, 4, upper, main, first, border, block, left, right, flux, held)
    leave(held, dens, press, vel, jnp.where(upper, WIDTH, 0), sems)


def z_rest_kernel(
    bounds, main, second, border, dens_in, press_in, vel_in, dens, press, vel, flags, block, left, right, flux, held, sems
):
    del dens_in, press_in, vel_in
    upper = upper_first("gz")
    sweep_rest("gz", 4, bounds, flags, 4, upper, main, second, border, block, left, right, flux, held)
    leave(held, dens, press, vel, jnp.where(upper, 0, main.shape[1] - WIDTH), sems)


def swap(block, places):
    rows = lax.axis_size("row")
    pairs = []
    for (g, r), (h, q) in places:
        pairs += [(g * rows + r, h * rows + q), (h * rows + q, g * rows + r)]
    return lax.ppermute(block, ("gz", "row"), pairs)


def row_swap(block, turn):
    places = []
    for g in range(lax.axis_size("gz")):
        start = turn if g // RING in ROW_LATE else 1 - turn
        places += [((g, r), (g, r + 1)) for r in range(start, lax.axis_size("row") - 1, 2)]
    return swap(block, places)


def gz_swap(block, turn):
    places = [
        ((g, r), (g + 1, r))
        for g in range(turn, lax.axis_size("gz") - 1, 2)
        for r in range(lax.axis_size("row"))
    ]
    return swap(block, places)


def on_device(density, pressure, velocity, boundary):
    planes, rows, cells = density.shape
    half = cells // LANES
    f32 = jnp.float32
    hbm = pl.BlockSpec(memory_space=pltpu.HBM)
    flags = pltpu.SMEM((6,), jnp.int32)
    vmem = pl.BlockSpec(memory_space=pltpu.VMEM)
    params = pltpu.CompilerParams(vmem_limit_bytes=32 << 20)
    by_y = jax.ShapeDtypeStruct((5, rows, planes, cells), f32)
    by_z = jax.ShapeDtypeStruct((5, planes, rows, cells), f32)
    y_edge = jax.ShapeDtypeStruct((5, WIDTH, planes, cells), f32)
    z_edge = jax.ShapeDtypeStruct((5, WIDTH, rows, cells), f32)
    turn = pltpu.VMEM((5 * half * planes * rows, LANES), f32)

    def part_work(inner, faces, whole, done):
        return [
            flags,
            pltpu.VMEM((5, whole, inner, cells), f32),
            pltpu.VMEM((5, faces, inner, cells), f32),
            pltpu.VMEM((5, faces, inner, cells), f32),
            pltpu.VMEM((5, done + 1, inner, cells), f32),
        ]

    main, first, second = pl.pallas_call(
        x_kernel,
        out_shape=(by_y, y_edge, y_edge),
        in_specs=[hbm, hbm, hbm, hbm],
        out_specs=(vmem, vmem, vmem),
        scratch_shapes=[
            pltpu.VMEM((5, planes, rows, cells), f32),
            flags,
            pltpu.SemaphoreType.DMA((6,)),
            pltpu.VMEM((5, planes * rows, cells), f32),
            pltpu.VMEM((5, planes * rows, cells), f32),
            pltpu.VMEM((5, planes * rows, LANES), f32),
            turn,
        ],
        compiler_params=params,
        name="x_sweep",
    )(*(pltpu.with_memory_space_constraint(a, pltpu.HBM) for a in (boundary, density, pressure, velocity)))
    first = row_swap(first, 0)
    second = row_swap(second, 1)
    most = rows - WIDTH
    done, border = pl.pallas_call(
        y_most_kernel,
        out_shape=(
            jax.ShapeDtypeStruct((5, most, planes, cells), f32),
            jax.ShapeDtypeStruct((5, planes, cells), f32),
        ),
        in_specs=[hbm, vmem, vmem],
        out_specs=(vmem, vmem),
        scratch_shapes=part_work(planes, most + 1, rows + WIDTH, most),
        compiler_params=params,
        name="y_sweep_most",
    )(boundary, main, first)
    main, first, second = pl.pallas_call(
        y_rest_kernel,
        out_shape=(by_z, z_edge, z_edge),
        in_specs=[hbm, vmem, vmem, vmem, vmem],
        out_specs=(vmem, vmem, vmem),
        scratch_shapes=part_work(planes, WIDTH, rows, WIDTH)
        + [pltpu.VMEM((5, WIDTH, planes, cells), f32), turn],
        compiler_params=params,
        name="y_sweep_rest",
    )(boundary, main, second, border, done)
    first = gz_swap(first, 0)
    second = gz_swap(second, 1)
    results = (
        jax.ShapeDtypeStruct(density.shape, f32),
        jax.ShapeDtypeStruct(pressure.shape, f32),
        jax.ShapeDtypeStruct(velocity.shape, f32),
    )

    def z_work(faces, whole, done):
        return part_work(rows, faces, whole, done) + [
            pltpu.VMEM((5, done, rows, cells), f32),
            pltpu.SemaphoreType.DMA((5,)),
        ]

    most = planes - WIDTH
    *partial, border = pl.pallas_call(
        z_most_kernel,
        out_shape=results + (jax.ShapeDtypeStruct((5, rows, cells), f32),),
        in_specs=[hbm, vmem, vmem],
        out_specs=(hbm, hbm, hbm, vmem),
        scratch_shapes=z_work(most + 1, planes + WIDTH, most),
        compiler_params=params,
        name="z_sweep_most",
    )(boundary, main, first)
    return pl.pallas_call(
        z_rest_kernel,
        out_shape=results,
        in_specs=[hbm, vmem, vmem, vmem, hbm, hbm, hbm],
        out_specs=(hbm, hbm, hbm),
        scratch_shapes=z_work(WIDTH, planes, WIDTH),
        input_output_aliases={4: 0, 5: 1, 6: 2},
        compiler_params=params,
        name="z_sweep_rest",
    )(boundary, main, second, border, *partial)


def solution(mesh):
    in_specs = (P("gz", "row", None), P("gz", "row", None), P(None, "gz", "row", None), P())
    out_specs = (P("gz", "row", None), P("gz", "row", None), P(None, "gz", "row", None))
    return jax.shard_map(
        on_device, mesh=mesh, in_specs=in_specs, out_specs=out_specs, check_vma=False
    )
```
